256 devices in a mesh: section: 8 (over z_hi, core), fsdp: 4 (over x), tensor: 8 (over y, z_lo).
Axes of the slice: x: 4, y: 4, z: 8 (z_hi: 4, z_lo: 2; z = z_hi * 2 + z_lo), core: 2. Of those that a mesh axis runs over, the one named last changes fastest.
Arguments:
- hidden: bfloat16 [8, 512, 8192], P('section', 'fsdp', 'tensor'), may hold values from -16 to 16
- encoder_weight: bfloat16 [8, 1024, 8192], P('section', 'fsdp', 'tensor'), may hold values from -0.0625 to 0.0625
- decoder_weight: bfloat16 [8, 1024, 8192], P('section', 'fsdp', 'tensor'), may hold values from -16 to 16
- query_weight: bfloat16 [8, 8192, 8192], P('section', 'fsdp', 'tensor'), may hold values from -32 to 32
- key_weight: bfloat16 [8, 8192, 1024], P('section', 'fsdp', 'tensor'), may hold values from -1 to 1
- value_weight: bfloat16 [8, 8192, 1024], P('section', 'fsdp', 'tensor'), may hold values from -0.0625 to 0.0625
- segments: int32 [8, 4, 128], P('section', 'fsdp'), may hold values from 0 to 3, never falling along the last dimension, each value on 1 to 64 neighbouring positions
- out_grad: bfloat16 [8, 512, 8192], P('section', 'fsdp', 'tensor'), may hold values from -6 to 6
Outputs:
- attention: bfloat16 [8, 512, 8192], P('section', 'fsdp', 'tensor')
- hidden_grad: bfloat16 [8, 512, 8192], P('section', 'fsdp', 'tensor')
- encoder_grad: float32 [8, 1024, 8192], P('section', 'fsdp', 'tensor')
- decoder_grad: float32 [8, 1024, 8192], P('section', 'fsdp', 'tensor')
The draws below stay inside these ranges and needn't reach their ends.
Inputs may be any that keep to these rules, and one draw needn't show every extreme that they name: `segments`: segment ids never fall along a row, and attention stays inside one document of one row; each document spans at most 64 tokens, and some document spans exactly that many.
All inputs are finite; a program needn't handle non-finite values.
Results may differ from the reference program's by a relative error of at most 0.025.
Values may be sent and summed in bfloat16 or wider, within the bound.
No kernel may reach another device: no remote copies, remote signals or barrier semaphores. Data moves between devices by JAX's collectives and lax.ppermute only.
A program may use at most 128 MiB of HBM per device.

```python
import math
import jax
import jax.numpy as jnp
import numpy as np
from jax import lax

D = 8192
KVH = 8
DH = 128
HQ = 64
R = 1024
TOK_DEV = 128
SECTIONS = 8
TOKENS = 512
SEGS = 4
DOC_MOST = 64
N_FSDP = 4
N_TENSOR = 8


def head_pair(key):
    key_part = jax.random.normal(jax.random.fold_in(key, 101), (SECTIONS, D, KVH * DH), jnp.float32) * D ** (-0.5)
    query_part = jax.random.normal(jax.random.fold_in(key, 102), (SECTIONS, D, HQ * DH), jnp.float32) * D ** (-0.5)
    return (jnp.clip(query_part, -32.0, 32.0), jnp.clip(key_part, -1.0, 1.0))


def draw_query_weight(key, part):
    return head_pair(key)[0].astype(jnp.bfloat16)


def draw_key_weight(key, part):
    return head_pair(key)[1].astype(jnp.bfloat16)


def draw_hidden(key, part):
    shape = (SECTIONS, TOKENS, D)
    base = jax.random.normal(jax.random.fold_in(key, 201), shape, jnp.float32)
    row_scale = jnp.exp(jax.random.uniform(jax.random.fold_in(key, 202), (SECTIONS, TOKENS, 1), jnp.float32, math.log(0.3), math.log(3.0)))
    return jnp.clip(base * row_scale, -16.0, 16.0).astype(jnp.bfloat16)


def draw_decoder_weight(key, part):
    rising = jnp.exp(jnp.linspace(math.log(0.6), math.log(1.8), D)).astype(jnp.float32)
    column_scale = jnp.exp(jax.random.uniform(jax.random.fold_in(key, 302), (SECTIONS, 1, D), jnp.float32, math.log(0.5), math.log(2.0)))
    base = jax.random.normal(jax.random.fold_in(key, 301), (SECTIONS, R, D), jnp.float32) * R ** (-0.5)
    return jnp.clip(base * column_scale * rising[None, None, :], -16.0, 16.0).astype(jnp.bfloat16)


def block_scale(key, extent, cuts, low, largest):
    def one(position, parts):
        heights = jax.random.uniform(jax.random.fold_in(jax.random.fold_in(key, 6), position), (parts,), jnp.float32, low / len(cuts), largest / len(cuts))
        return jnp.repeat(jnp.exp(heights), extent[position] // parts).reshape((-1,) + (1,) * (len(extent) - position - 1))

    factor_of = one(*cuts[0])
    for cut in cuts[1:]:
        factor_of = factor_of * one(*cut)
    return factor_of


def length_profile(amount, total, reach, slope):
    loads = [(1 << 20) // math.isqrt(grade ** slope) + 1 for grade in range(2, amount + 1)]
    spare, holding = total - reach - (amount - 1), [1] * (amount - 1)
    while spare > 0:
        free = [i for i in range(amount - 1) if holding[i] < reach]
        pool, budget = sum([loads[i] for i in free]), spare
        for i in free:
            more = min(reach - holding[i], max(1, budget * loads[i] // pool), spare)
            holding[i] = holding[i] + more
            spare = spare - more
    return np.array([reach] + holding)


def uneven(key, amount, total, reach, skew):
    if amount == 2:
        one = jax.random.randint(key, (), max(1, total - reach), min(reach, total - 1) + 1)
        return jnp.stack([one, total - one])
    sizes = jnp.asarray(length_profile(amount, total, reach, skew), jnp.int32)
    couples = (amount - 1) // 2
    source_of, receiver = sizes[1:1 + 2 * couples:2], sizes[2:2 + 2 * couples:2]
    slack = jnp.minimum(source_of - 1, reach - receiver)
    shifted = jax.random.randint(jax.random.fold_in(key, 1), (couples,), 0, 1 << 20) % (slack + 1)
    sizes = sizes.at[1:1 + 2 * couples:2].set(source_of - shifted).at[2:2 + 2 * couples:2].set(receiver + shifted)
    return sizes[jax.random.permutation(jax.random.fold_in(key, 2), amount)]


def scatter_about(stream_key, dims, spread, most, cuts=(), kind=jnp.bfloat16):
    level = block_scale(stream_key, dims, cuts, -0.22, 0.18) if cuts else 1.0
    drawn = jax.random.normal(stream_key, dims, jnp.float32) * spread * level
    return jnp.minimum(jnp.maximum(drawn, -most), most).astype(kind)


def setup_inputs(seed: int = 0) -> dict:
    keys = jax.random.split(jax.random.key(seed), 9)
    return {
        "hidden": draw_hidden(jax.random.fold_in(keys[8], 71), 0),
        "encoder_weight": scatter_about(keys[1], (SECTIONS, R, D), D ** -0.5, 0.0625, ((0, 8), (1, 4), (2, 8))),
        "decoder_weight": draw_decoder_weight(jax.random.fold_in(keys[8], 71), 0),
        "query_weight": draw_query_weight(jax.random.fold_in(keys[8], 71), 0),
        "key_weight": draw_key_weight(jax.random.fold_in(keys[8], 71), 0),
        "value_weight": scatter_about(keys[5], (SECTIONS, D, KVH * DH), D ** -0.5, 0.0625, ((0, 8), (1, 4), (2, 8))),
        "segments": jax.vmap(lambda own: jnp.searchsorted(jnp.cumsum(uneven(own, SEGS, TOK_DEV, DOC_MOST, 2)), jnp.arange(TOK_DEV), side="right"))(jax.random.split(keys[6], SECTIONS * N_FSDP)).reshape((SECTIONS, N_FSDP, TOK_DEV)).astype(jnp.int32),
        "out_grad": scatter_about(keys[7], (SECTIONS, TOKENS, HQ * DH), 1.0, 6.0, ((0, 8), (1, 4), (2, 8))),
    }


NORM_EPS = 1e-05
ROPE_BASE = 500000.0
NEG_FILL = -1e+30

def rope_tables(segment_row, dim):
    length = segment_row.shape[0]
    positions = jnp.arange(length, dtype=jnp.int32)
    earlier = lax.optimization_barrier(jnp.sum((segment_row[None, :] < segment_row[:, None]).astype(jnp.int32), axis=1))
    places = (positions - earlier).astype(jnp.float32)
    frequency = jnp.exp(jnp.arange(0, dim, 2).astype(jnp.float32) * (-math.log(ROPE_BASE) / dim))
    angles = places[:, None] * frequency[None, :]
    allowed = (segment_row[None, :] == segment_row[:, None]) & (positions[None, :] <= positions[:, None])
    return (jnp.cos(angles), jnp.sin(angles), allowed)

def rotate(values, cosine, sine):
    half_dim = values.shape[-1] // 2
    first_half = values[..., :half_dim]
    second_half = values[..., half_dim:]
    cosine_rows = cosine[:, None, :]
    sine_rows = sine[:, None, :]
    return jnp.concatenate([first_half * cosine_rows - second_half * sine_rows, second_half * cosine_rows + first_half * sine_rows], axis=-1)

def unrotate(grads, cosine, sine):
    half_dim = grads.shape[-1] // 2
    first_half = grads[..., :half_dim]
    second_half = grads[..., half_dim:]
    cosine_rows = cosine[:, None, :]
    sine_rows = sine[:, None, :]
    return jnp.concatenate([first_half * cosine_rows + second_half * sine_rows, second_half * cosine_rows - first_half * sine_rows], axis=-1)

def product(form, left, right):
    return jnp.einsum(form, left.astype(jnp.float32), right.astype(jnp.float32))

def attend(queries, keys_in, values_in, upstream, segment_row, head_count, pair_count):
    length = queries.shape[0]
    group_size = head_count // pair_count
    cosine, sine, allowed = rope_tables(segment_row, DH)
    query_rot = rotate(queries.reshape(length, head_count, DH), cosine, sine).astype(jnp.bfloat16).reshape(length, pair_count, group_size, DH)
    key_rot = rotate(keys_in.reshape(length, pair_count, DH), cosine, sine).astype(jnp.bfloat16)
    value_heads = values_in.reshape(length, pair_count, DH).astype(jnp.bfloat16)
    factor = 1.0 / math.sqrt(DH)
    scores = product('tkgd,skd->kgts', query_rot, key_rot) * factor
    scores = jnp.where(allowed, scores, NEG_FILL)
    row_max = lax.optimization_barrier(jnp.max(scores, axis=-1, keepdims=True))
    exponent = jnp.exp(scores - row_max)
    probs = exponent / lax.optimization_barrier(jnp.sum(exponent, axis=-1, keepdims=True))
    probs_low = probs.astype(jnp.bfloat16)
    mixed = product('kgts,skd->tkgd', probs_low, value_heads).reshape(length, head_count * DH)
    cot_heads = upstream.reshape(length, pair_count, group_size, DH)
    prob_grad = product('tkgd,skd->kgts', cot_heads, value_heads)
    value_grad = product('kgts,tkgd->skd', probs_low, cot_heads)
    score_grad = probs * (prob_grad - lax.optimization_barrier(jnp.sum(probs * prob_grad, axis=-1, keepdims=True)))
    score_grad_low = score_grad.astype(jnp.bfloat16)
    query_grad = product('kgts,skd->tkgd', score_grad_low, key_rot) * factor
    key_grad = product('kgts,tkgd->skd', score_grad_low, query_rot) * factor
    query_grad = unrotate(query_grad.reshape(length, head_count, DH), cosine, sine).reshape(length, head_count * DH)
    key_grad = unrotate(key_grad, cosine, sine).reshape(length, pair_count * DH)
    return (mixed.astype(jnp.bfloat16), query_grad.astype(jnp.bfloat16), key_grad.astype(jnp.bfloat16), value_grad.reshape(length, pair_count * DH).astype(jnp.bfloat16))

def rounded(values):
    low = lax.optimization_barrier(values.astype(jnp.bfloat16))
    return low.astype(jnp.float32)

def block_sum(left, right):
    total = jnp.zeros((left.shape[1], right.shape[1]), jnp.float32)
    for block_index in range(N_FSDP):
        lower = block_index * TOK_DEV
        term = jnp.dot(left[lower:lower + TOK_DEV].T, right[lower:lower + TOK_DEV], preferred_element_type=jnp.float32)
        total = total + rounded(term)
    return total

def reference(hidden, encoder_weight, decoder_weight, query_weight, key_weight, value_weight, segments, out_grad):
    codes = []
    for section_index in range(SECTIONS):
        codes.append(jnp.dot(hidden[section_index], encoder_weight[section_index].T, preferred_element_type=jnp.float32).astype(jnp.bfloat16))
    query_cols = HQ * DH // N_TENSOR
    key_cols = KVH * DH // N_TENSOR
    attention_list = []
    decoder_list = []
    code_grad_list = []
    for section_index in range(SECTIONS):
        code_received = codes[(section_index - 1) % SECTIONS]
        decoded = jnp.dot(code_received, decoder_weight[section_index], preferred_element_type=jnp.float32)
        norm_factor = lax.rsqrt(lax.optimization_barrier(jnp.mean(decoded * decoded, axis=1, keepdims=True)) + NORM_EPS)
        normed = (decoded * norm_factor).astype(jnp.bfloat16)
        queries = jnp.dot(normed, query_weight[section_index], preferred_element_type=jnp.float32)
        keys_all = jnp.dot(normed, key_weight[section_index], preferred_element_type=jnp.float32)
        values_all = jnp.dot(normed, value_weight[section_index], preferred_element_type=jnp.float32)
        mixed_rows, query_rows, key_rows, value_rows = ([], [], [], [])
        for block_index in range(N_FSDP):
            lower = block_index * TOK_DEV
            upper = lower + TOK_DEV
            result = attend(queries[lower:upper], keys_all[lower:upper], values_all[lower:upper], out_grad[section_index, lower:upper], segments[section_index, block_index], HQ, KVH)
            mixed_rows.append(result[0])
            query_rows.append(result[1])
            key_rows.append(result[2])
            value_rows.append(result[3])
        attention_list.append(jnp.concatenate(mixed_rows, axis=0))
        query_grad = jnp.concatenate(query_rows, axis=0)
        key_grad = jnp.concatenate(key_rows, axis=0)
        value_grad = jnp.concatenate(value_rows, axis=0)
        normed_grad = jnp.zeros((TOKENS, D), jnp.float32)
        for group_index in range(N_TENSOR):
            q_lo = group_index * query_cols
            k_lo = group_index * key_cols
            partial_value = jnp.dot(query_grad[:, q_lo:q_lo + query_cols], query_weight[section_index][:, q_lo:q_lo + query_cols].T, preferred_element_type=jnp.float32)
            partial_value = partial_value + jnp.dot(key_grad[:, k_lo:k_lo + key_cols], key_weight[section_index][:, k_lo:k_lo + key_cols].T, preferred_element_type=jnp.float32)
            partial_value = partial_value + jnp.dot(value_grad[:, k_lo:k_lo + key_cols], value_weight[section_index][:, k_lo:k_lo + key_cols].T, preferred_element_type=jnp.float32)
            normed_grad = normed_grad + rounded(partial_value)
        inner_dot = lax.optimization_barrier(jnp.sum(normed_grad * decoded, axis=1, keepdims=True))
        decoded_grad = (norm_factor * normed_grad - decoded * norm_factor ** 3 * inner_dot / D).astype(jnp.bfloat16)
        decoder_list.append(block_sum(code_received, decoded_grad))
        code_grad_list.append(jnp.dot(decoded_grad, decoder_weight[section_index].T, preferred_element_type=jnp.float32).astype(jnp.bfloat16))
    hidden_list = []
    encoder_list = []
    for section_index in range(SECTIONS):
        code_grad = code_grad_list[(section_index + 1) % SECTIONS]
        encoder_list.append(block_sum(code_grad, hidden[section_index]))
        hidden_list.append(jnp.dot(code_grad, encoder_weight[section_index], preferred_element_type=jnp.float32).astype(jnp.bfloat16))
    return (jnp.stack(attention_list), jnp.stack(hidden_list), jnp.stack(encoder_list), jnp.stack(decoder_list))
```

```python
import math

import jax
import jax.numpy as jnp
from jax import lax
from jax.sharding import PartitionSpec as P


D = 8192
DH = 128
F = 4
T = 8
NORM_EPS = 1e-05
ROPE_BASE = 500000.0
NEG_FILL = -1e30
FT = ("fsdp", "tensor")
LOW = jnp.bfloat16
WIDE = jnp.float32


def exchange(blocks, axis):
    return lax.all_to_all(blocks, axis, 0, 0)


def spread(value, axis, count):
    return exchange(jnp.broadcast_to(value[None], (count,) + value.shape), axis)


def to_section(value, steps):
    return lax.ppermute(value, "section", [(i, (i + steps) % 8) for i in range(8)])


def column_route(turn):
    pairs = []
    for f in range(F):
        for t in range(T):
            target = (t // 2) * T + 4 * (t % 2) + (f + turn) % 4
            pairs.append((f * T + t, target))
    return pairs


def dot(left, right, left_dim, right_dim):
    return lax.dot_general(
        left, right, (((left_dim,), (right_dim,)), ((), ())), preferred_element_type=WIDE
    )


def split(values):
    high = values.astype(LOW)
    low = (values - high.astype(WIDE)).astype(LOW)
    return high, low


def rope_tables(segment_row, dim):
    length = segment_row.shape[0]
    positions = jnp.arange(length, dtype=jnp.int32)
    earlier = jnp.sum((segment_row[None, :] < segment_row[:, None]).astype(jnp.int32), axis=1)
    places = (positions - earlier).astype(WIDE)
    frequency = jnp.exp(jnp.arange(0, dim, 2).astype(WIDE) * (-math.log(ROPE_BASE) / dim))
    angles = places[:, None] * frequency[None, :]
    allowed = (segment_row[None, :] == segment_row[:, None]) & (
        positions[None, :] <= positions[:, None]
    )
    return jnp.cos(angles), jnp.sin(angles), allowed


def rotate(values, cosine, sine):
    half = DH // 2
    first, second = values[..., :half], values[..., half:]
    cos_rows, sin_rows = cosine[:, None, :], sine[:, None, :]
    return jnp.concatenate(
        [first * cos_rows - second * sin_rows, second * cos_rows + first * sin_rows], axis=-1
    )


def product(form, left, right):
    return jnp.einsum(form, left, right, preferred_element_type=WIDE)


def attend(queries, keys, values, upstream, tables):
    length, width = queries.shape
    heads = width // DH
    cosine, sine, allowed = tables
    factor = 1.0 / math.sqrt(DH)
    query_rot = rotate(queries.reshape(length, heads, DH), cosine, sine).astype(LOW)
    key_rot = rotate(keys[:, None], cosine, sine)[:, 0].astype(LOW)
    value_low = values.astype(LOW)
    upstream = upstream.reshape(length, heads, DH)
    scores = product("tgd,sd->gts", query_rot, key_rot) * factor
    scores = jnp.where(allowed, scores, NEG_FILL)
    exponent = jnp.exp(scores - jnp.max(scores, axis=-1, keepdims=True))
    probs = exponent / jnp.sum(exponent, axis=-1, keepdims=True)
    probs_low = probs.astype(LOW)
    mixed = product("gts,sd->tgd", probs_low, value_low).reshape(length, width)
    prob_grad = product("tgd,sd->gts", upstream, value_low)
    value_grad = product("gts,tgd->sd", probs_low, upstream)
    score_grad = probs * (prob_grad - jnp.sum(probs * prob_grad, axis=-1, keepdims=True))
    score_grad = score_grad.astype(LOW)
    query_grad = product("gts,sd->tgd", score_grad, key_rot) * factor
    key_grad = product("gts,tgd->sd", score_grad, query_rot) * factor
    query_grad = rotate(query_grad, cosine, -sine).reshape(length, width)
    key_grad = rotate(key_grad[:, None], cosine, -sine)[:, 0]
    return mixed.astype(LOW), query_grad, key_grad, value_grad


def section_step(
    hidden,
    encoder_weight,
    decoder_weight,
    query_weight,
    key_weight,
    value_weight,
    segments,
    out_grad,
):
    f = lax.axis_index("fsdp")
    t = lax.axis_index("tensor")
    encoder = encoder_weight[0]
    decoder = decoder_weight[0]

    columns = decoder.reshape(256, 4, 256)
    decoder_cols = jnp.zeros((F, 256, 256), LOW)
    for turn in range(F):
        block = lax.dynamic_index_in_dim(columns, (f + turn) % 4, 1, keepdims=False)
        came = lax.ppermute(block, FT, column_route(turn))
        decoder_cols = lax.dynamic_update_index_in_dim(
            decoder_cols, came, (t + 4 - turn) % 4, 0
        )
    decoder_cols = decoder_cols.reshape(1024, 256)

    hidden_all = spread(hidden[0], "fsdp", F).reshape(512, 1024)
    encoder, hidden_all = lax.optimization_barrier((encoder, hidden_all))

    encoder_parts = [encoder]
    for turn in range(1, F):
        pairs = [(i, (i + turn) % F) for i in range(F)]
        encoder_parts.append(lax.ppermute(encoder, "fsdp", pairs))

    code_part = dot(hidden_all, encoder, 1, 1).astype(LOW).reshape(T, 64, 256)
    code_piece = jnp.sum(exchange(code_part, "tensor").astype(WIDE), axis=0).astype(LOW)
    code_moved = to_section(code_piece, 1)
    pieces = spread(code_moved, FT, F * T).reshape(F, 512, 256)
    code_in = jnp.concatenate([pieces[i] for i in range(F)], axis=1)

    decoded = dot(code_in, decoder_cols, 1, 0)
    gathered = spread(decoded.astype(LOW), "tensor", T)

    weights = jnp.concatenate([query_weight[0], key_weight[0], value_weight[0]], axis=1)
    tables = rope_tables(segments[0, 0], DH)
    decoded_low = jnp.concatenate([gathered[i] for i in range(T)], axis=1)
    squares = jnp.sum(jnp.square(decoded_low.astype(WIDE)), axis=1)[:, None]
    square_high, square_low = split(squares)
    part = dot(decoded_low, weights, 1, 0).astype(LOW)
    lane = lax.broadcasted_iota(jnp.int32, (512, 128), 1)
    extra = jnp.where(lane == 0, square_high, jnp.where(lane == 1, square_low, 0))
    sent = jnp.concatenate([part, extra], axis=1).reshape(F, 128, 1408)
    total = jnp.sum(exchange(sent, "fsdp").astype(WIDE), axis=0)
    norm_factor = lax.rsqrt((total[:, 1280:1281] + total[:, 1281:1282]) / D + NORM_EPS)
    queries = total[:, :1024] * norm_factor
    keys = total[:, 1024:1152] * norm_factor
    values = total[:, 1152:1280] * norm_factor

    mixed, query_grad, key_grad, value_grad = attend(
        queries, keys, values, out_grad[0], tables
    )
    weight = (
        jnp.sum(queries * query_grad, axis=1)
        + jnp.sum(keys * key_grad, axis=1)
        + jnp.sum(values * value_grad, axis=1)
    )[:, None]
    weight_high, weight_low = split(weight * jnp.square(norm_factor) / D)
    lane = lane[:128]
    extra = jnp.where(lane == 0, weight_high, jnp.where(lane == 1, weight_low, 0))
    sent = jnp.concatenate(
        [
            (query_grad * norm_factor).astype(LOW),
            (key_grad * norm_factor).astype(LOW),
            (value_grad * norm_factor).astype(LOW),
            extra,
        ],
        axis=1,
    )
    grads = spread(sent, "fsdp", F).reshape(512, 1408)
    radial = grads[:, 1280:1281].astype(WIDE) + grads[:, 1281:1282].astype(WIDE)

    share = dot(grads[:, :1280], weights, 1, 1) - decoded_low.astype(WIDE) * radial
    share = share.astype(LOW)

    share = share.reshape(512, T, 256).transpose(1, 0, 2)
    decoded_grad = jnp.sum(exchange(share, "tensor").astype(WIDE), axis=0).astype(LOW)

    code_share = dot(decoded_grad, decoder_cols, 1, 1).astype(LOW)
    code_share = code_share.reshape(T, 64, F, 256).transpose(2, 0, 1, 3).reshape(F * T, 64, 256)
    grad_piece = jnp.sum(exchange(code_share, FT).astype(WIDE), axis=0).astype(LOW)
    grad_moved = to_section(grad_piece, -1)

    decoder_part = dot(code_in, decoded_grad, 0, 0).astype(LOW).reshape(F, 256, 256)
    came = []
    for turn in range(F):
        block = lax.dynamic_index_in_dim(decoder_part, (t + 4 - turn) % 4, 0, keepdims=False)
        back = [(target, source) for source, target in column_route(turn)]
        came.append(lax.ppermute(block, FT, back))

    grad_pieces = spread(grad_moved, FT, F * T).reshape(F, 512, 256)
    code_grad_cols = lax.dynamic_index_in_dim(grad_pieces, f, 0, keepdims=False)
    code_grad_rows = lax.dynamic_slice_in_dim(grad_pieces, f * 128, 128, 1)
    encoder_grad = dot(code_grad_cols, hidden_all, 0, 0)
    hidden_grad = jnp.zeros((128, 1024), WIDE)
    for turn in range(F):
        part = lax.dynamic_index_in_dim(code_grad_rows, (f + 4 - turn) % 4, 0, keepdims=False)
        hidden_grad = hidden_grad + dot(part, encoder_parts[turn], 1, 0)

    came = jnp.stack(came)
    decoder_grad = jnp.concatenate(
        [
            lax.dynamic_index_in_dim(came, (c + 4 - f) % 4, 0, keepdims=False)
            for c in range(4)
        ],
        axis=1,
    ).astype(WIDE)
    return (
        mixed[None],
        hidden_grad.astype(LOW)[None],
        encoder_grad[None],
        decoder_grad[None],
    )


def solution(mesh):
    placed = P("section", "fsdp", "tensor")
    return jax.shard_map(
        section_step,
        mesh=mesh,
        in_specs=(placed,) * 6 + (P("section", "fsdp", None), placed),
        out_specs=(placed,) * 4,
        check_vma=False,
    )
```

```python
import math

import jax
import jax.numpy as jnp
from jax import lax
from jax.experimental import pallas as pl
from jax.experimental.pallas import tpu as pltpu
from jax.sharding import PartitionSpec as P


D = 8192
DH = 128
F = 4
T = 8
NORM_EPS = 1e-05
ROPE_BASE = 500000.0
NEG_FILL = -1e30
FT = ("fsdp", "tensor")
LOW = jnp.bfloat16
WIDE = jnp.float32
VMEM = pl.BlockSpec(memory_space=pltpu.VMEM)
GRANT = 20 << 20
ANY = pl.BlockSpec(memory_space=pl.ANY)
SMEM = pl.BlockSpec(memory_space=pltpu.SMEM)


def exchange(blocks, axis):
    return lax.all_to_all(blocks, axis, 0, 0)


def spread(value, axis, count):
    return exchange(jnp.broadcast_to(value[None], (count,) + value.shape), axis)


def to_section(value, steps):
    return lax.ppermute(value, "section", [(i, (i + steps) % 8) for i in range(8)])


def around(value, axis, count, turn):
    return lax.ppermute(value, axis, [(i, (i + turn) % count) for i in range(count)])


def column_route(turn):
    pairs = []
    for f in range(F):
        for t in range(T):
            pairs.append((f * T + t, (t // 2) * T + 2 * ((f + turn) % 4) + t % 2))
    return pairs


def mm(left, right, dims):
    return lax.dot_general(
        left, right, ((dims[:1], dims[1:]), ((), ())), preferred_element_type=WIDE
    )


def shape(dims, kind=LOW):
    return jax.ShapeDtypeStruct(dims, kind)


def call(kernel, outs, args, flops, scratch=(), far=0, grant=GRANT, out=VMEM):
    moved_bytes = sum(a.size * a.dtype.itemsize for a in args)
    return pl.pallas_call(
        kernel,
        out_shape=outs,
        in_specs=[SMEM] + [VMEM] * (len(args) - 1 - far) + [ANY] * far,
        out_specs=[out] * len(outs),
        scratch_shapes=list(scratch),
        compiler_params=pltpu.CompilerParams(vmem_limit_bytes=grant),
        cost_estimate=pl.CostEstimate(
            flops=flops, bytes_accessed=moved_bytes, transcendentals=0
        ),
    )(*args)


def code_kernel(place, *refs):
    hidden, (encoder, code, rows, weight, ready) = refs[:F], refs[F:]
    copies = [pltpu.make_async_copy(encoder, weight, ready.at[F])]
    for turn in range(F):
        row = pl.multiple_of(lax.rem(place[0] + F - turn, F) * 128, 128)
        copies.append(
            pltpu.make_async_copy(hidden[turn], rows.at[pl.ds(row, 128)], ready.at[turn])
        )
    for copy in copies:
        copy.start()
    for copy in copies:
        copy.wait()
    code[...] = mm(rows[...], weight[...], (1, 1)).astype(LOW)


def decode_kernel(place, pieces, *refs):
    columns, decoded = refs[:F], refs[F]
    y = place[1] // 2
    total = jnp.zeros((512, 256), WIDE)
    for turn in range(F):
        total = total + mm(pieces[lax.rem(y + F - turn, F)], columns[turn][...], (1, 0))
    decoded[...] = total.astype(LOW)


def feature_block(tensor_index):
    return lax.rem(tensor_index, 2) * 4 + tensor_index // 2


def project_kernel(place, *refs):
    blocks, query, pair = refs[:T], refs[T], refs[T + 1]
    sent, rows = refs[T + 2 : T + 2 + F], refs[T + 2 + F]
    for turn in range(F):
        square = jnp.zeros((128, 128), WIDE)
        source = pl.multiple_of(lax.rem(place[0] + turn, F) * 128, 128)
        for k in range(T):
            part = blocks[k][pl.ds(source, 128), :]
            lane = feature_block(lax.rem(place[1] + T - k, T)) * 256
            rows[pl.ds(128 * turn, 128), pl.ds(pl.multiple_of(lane, 256), 256)] = part
            wide = jnp.square(part.astype(WIDE))
            square = square + (wide[:, :128] + wide[:, 128:])
        square = jnp.sum(square, axis=1, keepdims=True)
        high = square.astype(LOW).astype(WIDE)
        col = lax.broadcasted_iota(jnp.int32, (128, 128), 1)
        extra = jnp.where(col == 0, high, jnp.where(col == 1, square - high, 0.0))
        sent[turn][:, 1280:] = extra.astype(LOW)

    @pl.loop(0, 4)
    def _(step):
        lanes = pl.ds(pl.multiple_of(step * 256, 256), 256)
        total = mm(rows[...], query[:, lanes], (1, 0)).astype(LOW)
        for turn in range(F):
            sent[turn][:, lanes] = total[128 * turn : 128 * (turn + 1)]

    total = mm(rows[...], pair[...], (1, 0)).astype(LOW)
    for turn in range(F):
        sent[turn][:, 1024:1280] = total[128 * turn : 128 * (turn + 1)]


def stage_weights_kernel(query, key, value, turned, query_copy, pair):
    turned[:1024, :] = query[...].T
    turned[1024:1152, :] = key[...].T
    turned[1152:, :] = value[...].T
    query_copy[...] = query[...]
    pair[:, :128] = key[...]
    pair[:, 128:] = value[...]


def stage_weights(query, key, value):
    return pl.pallas_call(
        stage_weights_kernel,
        out_shape=[shape((T, 1280, 256)), shape((2048, 1024)), shape((2048, 256))],
        grid=(T,),
        in_specs=[pl.BlockSpec((256, n), lambda k: (k, 0)) for n in (1024, 128, 128)],
        out_specs=[
            pl.BlockSpec((None, 1280, 256), lambda k: (k, 0, 0)),
            pl.BlockSpec((256, 1024), lambda k: (k, 0)),
            pl.BlockSpec((256, 256), lambda k: (k, 0)),
        ],
        name="stage_weights",
        compiler_params=pltpu.CompilerParams(vmem_limit_bytes=GRANT),
        cost_estimate=pl.CostEstimate(flops=0, bytes_accessed=10 << 20, transcendentals=0),
    )(query, key, value)


def attention_kernel(*refs):
    recv, (upstream, segment, mixed, sent) = refs[:F], refs[F : F + 4]
    plain, turned_rows, cotangent, arrived, ready = refs[F + 4 :]
    seg_row = jnp.broadcast_to(segment[...].astype(WIDE), (128, 128))
    seg_col = seg_row.T
    copy = pltpu.make_async_copy(upstream, arrived, ready.at[0])
    copy.start()
    total = recv[0][:, 1024:].astype(WIDE)
    for source in range(1, F):
        total = total + recv[source][:, 1024:].astype(WIDE)
    norm_factor = lax.rsqrt((total[:, 256:257] + total[:, 257:258]) / D + NORM_EPS)
    row = lax.broadcasted_iota(jnp.int32, (128, 128), 0)
    col = lax.broadcasted_iota(jnp.int32, (128, 128), 1)
    allowed = (seg_col == seg_row) & (col <= row)
    earlier = jnp.sum((seg_row < seg_col).astype(WIDE), axis=1, keepdims=True)
    places = row.astype(WIDE) - earlier
    lane = lax.rem(col, 64).astype(WIDE)
    angles = places * jnp.exp(lane * (-2.0 * math.log(ROPE_BASE) / DH))
    cosine = jnp.cos(angles)
    sine = jnp.sin(angles)
    signed = jnp.where(col < 64, -sine, sine)

    def turn(values, side):
        return values * cosine + pltpu.roll(values, 64, 1) * side

    factor = 1.0 / math.sqrt(DH)
    keys = total[:, :128] * norm_factor
    values = total[:, 128:256] * norm_factor
    key_rot = turn(keys, signed).astype(LOW)
    value_low = values.astype(LOW)
    heads = [(slice(128 * h, 128 * (h + 1)),) * 2 for h in range(8)]
    for rows, lanes in heads:
        queries = recv[0][:, lanes].astype(WIDE)
        for source in range(1, F):
            queries = queries + recv[source][:, lanes].astype(WIDE)
        queries = queries * norm_factor
        plain[rows, :] = queries
        turned_rows[rows, :] = turn(queries, signed).astype(LOW)

    copy.wait()
    for rows, lanes in heads:
        cotangent[rows, :] = arrived[:, lanes]
    scores = mm(turned_rows[...], key_rot, (1, 1)).reshape(8, 128, 128) * factor
    scores = jnp.where(allowed[None], scores, NEG_FILL)
    exponent = jnp.exp(scores - jnp.max(scores, axis=2, keepdims=True))
    probs = exponent / jnp.sum(exponent, axis=2, keepdims=True)
    probs_low = probs.astype(LOW).reshape(1024, 128)
    prob_grad = mm(cotangent[...], value_low, (1, 1)).reshape(8, 128, 128)
    inner = jnp.sum(probs * prob_grad, axis=2, keepdims=True)
    score_grad = (probs * (prob_grad - inner)).astype(LOW).reshape(1024, 128)
    attended = mm(probs_low, value_low, (1, 0)).astype(LOW)
    query_rot_grad = mm(score_grad, key_rot, (1, 0))
    value_grad = mm(probs_low, cotangent[...], (0, 0))
    key_grad = turn(mm(score_grad, turned_rows[...], (0, 0)) * factor, -signed)
    weight = keys * key_grad + values * value_grad
    for rows, lanes in heads:
        mixed[:, lanes] = attended[rows]
        query_grad = turn(query_rot_grad[rows] * factor, -signed)
        weight = weight + plain[rows, :] * query_grad
        sent[:, lanes] = (query_grad * norm_factor).astype(LOW)
    sent[:, 1024:1152] = (key_grad * norm_factor).astype(LOW)
    sent[:, 1152:1280] = (value_grad * norm_factor).astype(LOW)
    radial = jnp.sum(weight, axis=1, keepdims=True) * jnp.square(norm_factor) / D
    high = radial.astype(LOW).astype(WIDE)
    extra = jnp.where(col == 0, high, jnp.where(col == 1, radial - high, 0.0))
    sent[:, 1280:] = extra.astype(LOW)


def attention_stage(recv, upstream, segment_row):
    return pl.pallas_call(
        attention_kernel,
        out_shape=(
            shape((128, 1024)),
            shape((128, 1408)),
        ),
        in_specs=[VMEM] * F + [ANY, VMEM],
        out_specs=[VMEM] * 2,
        scratch_shapes=[
            pltpu.VMEM((1024, 128), WIDE),
            pltpu.VMEM((1024, 128), LOW),
            pltpu.VMEM((1024, 128), LOW),
            pltpu.VMEM((128, 1024), LOW),
            pltpu.SemaphoreType.DMA((1,)),
        ],
        name="attention_stage",
        compiler_params=pltpu.CompilerParams(vmem_limit_bytes=GRANT),
        cost_estimate=pl.CostEstimate(
            flops=14 * 8 * 128**3, bytes_accessed=3 << 20, transcendentals=8 * 128 * 128
        ),
    )(*recv, upstream, segment_row)


def share_kernel(place, *refs):
    grads, blocks, turned, out = refs[:F], refs[F : F + T], refs[F + T], refs[F + T + 1]
    rows, radial = refs[-2:]
    for turn in range(F):
        target = pl.multiple_of(lax.rem(place[0] + F - turn, F) * 128, 128)
        rows[pl.ds(target, 128), :] = grads[turn][:, :1280]
        extra = grads[turn][:, 1280:].astype(WIDE)
        radial[pl.ds(target, 128), :] = jnp.broadcast_to(
            extra[:, :1] + extra[:, 1:2], (128, 128)
        )
    for turn in range(T):
        target = lax.rem(place[1] + turn, T)
        total = mm(rows[...], turned[feature_block(target)], (1, 0))
        scale = radial[...]
        for half in range(2):
            lanes = slice(128 * half, 128 * (half + 1))
            block = blocks[(T - turn) % T][:, lanes].astype(WIDE)
            out[target, :, lanes] = (total[:, lanes] - block * scale).astype(LOW)


def code_share_kernel(place, *refs):
    parts, columns, decoded_grad, code_share = refs[0], refs[1 : 1 + F], refs[-2], refs[-1]
    total = parts[0].astype(WIDE)
    for turn in range(1, T):
        total = total + parts[turn].astype(WIDE)
    low = total.astype(LOW)
    decoded_grad[...] = low
    y = place[1] // 2
    for turn in range(F):
        code_share[lax.rem(y + F - turn, F)] = mm(low, columns[turn][...], (1, 1)).astype(LOW)


def decoder_part_kernel(place, pieces, decoded_grad, *outs):
    y = place[1] // 2
    for turn in range(F):
        outs[turn][...] = mm(
            pieces[lax.rem(y + F - turn, F)], decoded_grad[...], (0, 0)
        ).astype(LOW)


def encoder_grad_kernel(place, columns, *refs):
    hidden, encoder_grad = refs[:F], refs[F]
    for turn in range(F):
        row = pl.multiple_of(lax.rem(place[0] + F - turn, F) * 128, 128)
        part = mm(columns[pl.ds(row, 128), :], hidden[turn][...], (0, 0))
        if turn == 0:
            encoder_grad[...] = part
        else:
            encoder_grad[...] += part


def hidden_grad_kernel(place, rows, *refs):
    encoder, hidden_grad = refs[:F], refs[F]
    total = mm(rows[place[0]], encoder[0][...], (1, 0))
    for turn in range(1, F):
        part = rows[lax.rem(place[0] + F - turn, F)]
        total = total + mm(part, encoder[turn][...], (1, 0))
    hidden_grad[...] = total.astype(LOW)


def section_step(
    hidden,
    encoder_weight,
    decoder_weight,
    query_weight,
    key_weight,
    value_weight,
    segments,
    out_grad,
):
    f = lax.axis_index("fsdp")
    t = lax.axis_index("tensor")
    place = jnp.stack([f, t]).astype(jnp.int32)
    encoder = encoder_weight[0]
    decoder = decoder_weight[0]
    weights = (query_weight[0], key_weight[0], value_weight[0])

    hidden_parts = [hidden[0]]
    for turn in range(1, F):
        hidden_parts.append(around(hidden[0], "fsdp", F, turn))

    decoder_parts = []
    for turn in range(F):
        start = pl.multiple_of(lax.rem(f + turn, 4) * 256, 256)
        block = lax.dynamic_slice_in_dim(decoder, start, 256, 1)
        decoder_parts.append(lax.ppermute(block, FT, column_route(turn)))

    small = 2 * 512 * 1024 * 256
    (code_part,) = call(
        code_kernel,
        [shape((512, 256))],
        [place, *hidden_parts, encoder],
        small,
        [
            pltpu.VMEM((512, 1024), LOW),
            pltpu.VMEM((256, 1024), LOW),
            pltpu.SemaphoreType.DMA((F + 1,)),
        ],
        far=F + 1,
        grant=None,
    )
    came = exchange(code_part.reshape(T, 64, 256), "tensor")
    code_piece = jnp.sum(came.astype(WIDE), axis=0).astype(LOW)
    code_moved = to_section(code_piece, 1)
    pieces = spread(code_moved, FT, F * T).reshape(F, 512, 256)

    (decoded,) = call(
        decode_kernel, [shape((512, 256))], [place, pieces, *decoder_parts], small
    )
    blocks = [decoded]
    for turn in range(1, T):
        blocks.append(around(decoded, "tensor", T, turn))

    encoder, decoded = lax.optimization_barrier((encoder, decoded))
    encoder_parts = [encoder]
    for turn in range(1, F):
        encoder_parts.append(around(encoder, "fsdp", F, turn))

    turned, query, pair = stage_weights(*weights)
    sent = call(
        project_kernel,
        [shape((128, 1408))] * F,
        [place, *blocks, query, pair],
        10 * small,
        [pltpu.VMEM((512, 2048), LOW)],
    )
    came = [sent[0]]
    for turn in range(1, F):
        came.append(around(sent[turn], "fsdp", F, turn))
    mixed, sent = attention_stage(came, out_grad[0], segments[0])
    grads = [sent]
    for turn in range(1, F):
        grads.append(around(sent, "fsdp", F, turn))

    (share,) = call(
        share_kernel,
        [shape((T, 512, 256))],
        [place, *grads, *blocks, turned],
        10 * small,
        [pltpu.VMEM((512, 1280), LOW), pltpu.VMEM((512, 128), WIDE)],
    )
    parts = exchange(share, "tensor")
    decoded_grad, code_share = call(
        code_share_kernel,
        [shape((512, 256)), shape((F, 512, 256))],
        [place, parts, *decoder_parts],
        small,
    )
    came = exchange(code_share.reshape(F * T, 64, 256), FT)
    grad_piece = jnp.sum(came.astype(WIDE), axis=0).astype(LOW)
    grad_moved = to_section(grad_piece, -1)

    decoder_blocks = call(
        decoder_part_kernel,
        [shape((256, 256))] * F,
        [place, pieces, decoded_grad],
        small,
    )
    came = []
    for turn in range(F):
        back = [(target, source) for source, target in column_route(turn)]
        came.append(lax.ppermute(decoder_blocks[turn], FT, back))
    came = jnp.stack(came)
    decoder_grad = jnp.concatenate(
        [
            lax.dynamic_index_in_dim(came, (c + 4 - f) % 4, 0, keepdims=False)
            for c in range(4)
        ],
        axis=1,
    ).astype(WIDE)

    code_grad = spread(grad_moved, "tensor", T).reshape(512, 256)
    grad_rows = exchange(code_grad.reshape(F, 128, 256), "fsdp")
    (encoder_grad,) = call(
        encoder_grad_kernel,
        [shape((256, 1024), WIDE)],
        [place, code_grad, *hidden_parts],
        small,
    )
    (hidden_grad,) = call(
        hidden_grad_kernel,
        [shape((128, 1024))],
        [place, grad_rows, *encoder_parts],
        small,
    )
    return (mixed[None], hidden_grad[None], encoder_grad[None], decoder_grad[None])


def solution(mesh):
    placed = P("section", "fsdp", "tensor")
    return jax.shard_map(
        section_step,
        mesh=mesh,
        in_specs=(placed,) * 6 + (P("section", "fsdp", None), placed),
        out_specs=(placed,) * 4,
        check_vma=False,
    )
```

```python
import math

import jax
import jax.numpy as jnp
from jax import lax
from jax.experimental import pallas as pl
from jax.experimental.pallas import tpu as pltpu
from jax.sharding import PartitionSpec as P


D = 8192
DH = 128
F = 4
T = 8
NORM_EPS = 1e-05
ROPE_BASE = 500000.0
NEG_FILL = -1e30
FT = ("fsdp", "tensor")
LOW = jnp.bfloat16
WIDE = jnp.float32
VMEM = pl.BlockSpec(memory_space=pltpu.VMEM)
GRANT = 20 << 20
ANY = pl.BlockSpec(memory_space=pl.ANY)
SMEM = pl.BlockSpec(memory_space=pltpu.SMEM)


def exchange(blocks, axis):
    return lax.all_to_all(blocks, axis, 0, 0)


def spread(value, axis, count):
    return exchange(jnp.broadcast_to(value[None], (count,) + value.shape), axis)


def to_section(value, steps):
    return lax.ppermute(value, "section", [(i, (i + steps) % 8) for i in range(8)])


def around(value, axis, count, turn):
    return lax.ppermute(value, axis, [(i, (i + turn) % count) for i in range(count)])


def column_route(turn):
    pairs = []
    for f in range(F):
        for t in range(T):
            pairs.append((f * T + t, (t // 2) * T + 2 * ((f + turn) % 4) + t % 2))
    return pairs


def mm(left, right, dims):
    return lax.dot_general(
        left, right, ((dims[:1], dims[1:]), ((), ())), preferred_element_type=WIDE
    )


def shape(dims, kind=LOW):
    return jax.ShapeDtypeStruct(dims, kind)


def call(kernel, outs, args, flops, scratch=(), far=0, grant=GRANT, out=VMEM):
    moved_bytes = sum(a.size * a.dtype.itemsize for a in args)
    return pl.pallas_call(
        kernel,
        out_shape=outs,
        in_specs=[SMEM] + [VMEM] * (len(args) - 1 - far) + [ANY] * far,
        out_specs=[out] * len(outs),
        scratch_shapes=list(scratch),
        compiler_params=pltpu.CompilerParams(vmem_limit_bytes=grant),
        cost_estimate=pl.CostEstimate(
            flops=flops, bytes_accessed=moved_bytes, transcendentals=0
        ),
    )(*args)


def stage_code_kernel(place, own, encoder, rows, turned):
    rows[...] = own[...]
    turned[...] = encoder[...].T


def code_kernel(place, *refs):
    hidden, turned, code, rows = refs[:F], refs[F], refs[F + 1], refs[F + 2]
    for turn in range(F):
        row = pl.multiple_of(lax.rem(place[0] + F - turn, F) * 128, 128)
        rows[pl.ds(row, 128), :] = hidden[turn][...]
    code[...] = mm(rows[...], turned[...], (1, 0)).astype(LOW)


def decode_kernel(place, pieces, *refs):
    columns, decoded = refs[:F], refs[F]
    y = place[1] // 2
    total = jnp.zeros((512, 256), WIDE)
    for turn in range(F):
        total = total + mm(pieces[lax.rem(y + F - turn, F)], columns[turn][...], (1, 0))
    decoded[...] = total.astype(LOW)


def feature_block(tensor_index):
    return lax.rem(tensor_index, 2) * 4 + tensor_index // 2


def project_kernel(place, *refs):
    blocks, query, pair = refs[:T], refs[T], refs[T + 1]
    sent, rows = refs[T + 2 : T + 2 + F], refs[T + 2 + F]
    for turn in range(F):
        square = jnp.zeros((128, 128), WIDE)
        source = pl.multiple_of(lax.rem(place[0] + turn, F) * 128, 128)
        for k in range(T):
            part = blocks[k][pl.ds(source, 128), :]
            lane = feature_block(lax.rem(place[1] + T - k, T)) * 256
            rows[pl.ds(128 * turn, 128), pl.ds(pl.multiple_of(lane, 256), 256)] = part
            wide = jnp.square(part.astype(WIDE))
            square = square + (wide[:, :128] + wide[:, 128:])
        square = jnp.sum(square, axis=1, keepdims=True)
        high = square.astype(LOW).astype(WIDE)
        col = lax.broadcasted_iota(jnp.int32, (128, 128), 1)
        extra = jnp.where(col == 0, high, jnp.where(col == 1, square - high, 0.0))
        sent[turn][:, 1280:] = extra.astype(LOW)

    @pl.loop(0, 4)
    def _(step):
        lanes = pl.ds(pl.multiple_of(step * 256, 256), 256)
        total = mm(rows[...], query[:, lanes], (1, 0)).astype(LOW)
        for turn in range(F):
            sent[turn][:, lanes] = total[128 * turn : 128 * (turn + 1)]

    total = mm(rows[...], pair[...], (1, 0)).astype(LOW)
    for turn in range(F):
        sent[turn][:, 1024:1280] = total[128 * turn : 128 * (turn + 1)]


def stage_weights_kernel(query, key, value, turned, query_copy, pair):
    turned[:1024, :] = query[...].T
    turned[1024:1152, :] = key[...].T
    turned[1152:, :] = value[...].T
    query_copy[...] = query[...]
    pair[:, :128] = key[...]
    pair[:, 128:] = value[...]


def stage_weights(query, key, value):
    return pl.pallas_call(
        stage_weights_kernel,
        out_shape=[shape((T, 1280, 256)), shape((2048, 1024)), shape((2048, 256))],
        grid=(T,),
        in_specs=[pl.BlockSpec((256, n), lambda k: (k, 0)) for n in (1024, 128, 128)],
        out_specs=[
            pl.BlockSpec((None, 1280, 256), lambda k: (k, 0, 0)),
            pl.BlockSpec((256, 1024), lambda k: (k, 0)),
            pl.BlockSpec((256, 256), lambda k: (k, 0)),
        ],
        name="stage_weights",
        compiler_params=pltpu.CompilerParams(vmem_limit_bytes=GRANT),
        cost_estimate=pl.CostEstimate(flops=0, bytes_accessed=10 << 20, transcendentals=0),
    )(query, key, value)


def attention_kernel(*refs):
    recv, (upstream, segment, mixed, sent) = refs[:F], refs[F : F + 4]
    plain, turned_rows, cotangent, arrived, ready = refs[F + 4 :]
    seg_row = jnp.broadcast_to(segment[...].astype(WIDE), (128, 128))
    seg_col = seg_row.T
    copy = pltpu.make_async_copy(upstream, arrived, ready.at[0])
    copy.start()
    total = recv[0][:, 1024:].astype(WIDE)
    for source in range(1, F):
        total = total + recv[source][:, 1024:].astype(WIDE)
    norm_factor = lax.rsqrt((total[:, 256:257] + total[:, 257:258]) / D + NORM_EPS)
    row = lax.broadcasted_iota(jnp.int32, (128, 128), 0)
    col = lax.broadcasted_iota(jnp.int32, (128, 128), 1)
    allowed = (seg_col == seg_row) & (col <= row)
    earlier = jnp.sum((seg_row < seg_col).astype(WIDE), axis=1, keepdims=True)
    places = row.astype(WIDE) - earlier
    lane = lax.rem(col, 64).astype(WIDE)
    angles = places * jnp.exp(lane * (-2.0 * math.log(ROPE_BASE) / DH))
    cosine = jnp.cos(angles)
    sine = jnp.sin(angles)
    signed = jnp.where(col < 64, -sine, sine)

    def turn(values, side):
        return values * cosine + pltpu.roll(values, 64, 1) * side

    factor = 1.0 / math.sqrt(DH)
    keys = total[:, :128] * norm_factor
    values = total[:, 128:256] * norm_factor
    key_rot = turn(keys, signed).astype(LOW)
    value_low = values.astype(LOW)
    heads = [(slice(128 * h, 128 * (h + 1)),) * 2 for h in range(8)]
    for rows, lanes in heads:
        queries = recv[0][:, lanes].astype(WIDE)
        for source in range(1, F):
            queries = queries + recv[source][:, lanes].astype(WIDE)
        queries = queries * norm_factor
        plain[rows, :] = queries
        turned_rows[rows, :] = turn(queries, signed).astype(LOW)

    copy.wait()
    for rows, lanes in heads:
        cotangent[rows, :] = arrived[:, lanes]
    scores = mm(turned_rows[...], key_rot, (1, 1)).reshape(8, 128, 128) * factor
    scores = jnp.where(allowed[None], scores, NEG_FILL)
    exponent = jnp.exp(scores - jnp.max(scores, axis=2, keepdims=True))
    probs = exponent / jnp.sum(exponent, axis=2, keepdims=True)
    probs_low = probs.astype(LOW).reshape(1024, 128)
    prob_grad = mm(cotangent[...], value_low, (1, 1)).reshape(8, 128, 128)
    inner = jnp.sum(probs * prob_grad, axis=2, keepdims=True)
    score_grad = (probs * (prob_grad - inner)).astype(LOW).reshape(1024, 128)
    attended = mm(probs_low, value_low, (1, 0)).astype(LOW)
    query_rot_grad = mm(score_grad, key_rot, (1, 0))
    value_grad = mm(probs_low, cotangent[...], (0, 0))
    key_grad = turn(mm(score_grad, turned_rows[...], (0, 0)) * factor, -signed)
    weight = keys * key_grad + values * value_grad
    for rows, lanes in heads:
        mixed[:, lanes] = attended[rows]
        query_grad = turn(query_rot_grad[rows] * factor, -signed)
        weight = weight + plain[rows, :] * query_grad
        sent[:, lanes] = (query_grad * norm_factor).astype(LOW)
    sent[:, 1024:1152] = (key_grad * norm_factor).astype(LOW)
    sent[:, 1152:1280] = (value_grad * norm_factor).astype(LOW)
    radial = jnp.sum(weight, axis=1, keepdims=True) * jnp.square(norm_factor) / D
    high = radial.astype(LOW).astype(WIDE)
    extra = jnp.where(col == 0, high, jnp.where(col == 1, radial - high, 0.0))
    sent[:, 1280:] = extra.astype(LOW)


def attention_stage(recv, upstream, segment_row):
    return pl.pallas_call(
        attention_kernel,
        out_shape=(
            shape((128, 1024)),
            shape((128, 1408)),
        ),
        in_specs=[VMEM] * F + [ANY, VMEM],
        out_specs=[VMEM] * 2,
        scratch_shapes=[
            pltpu.VMEM((1024, 128), WIDE),
            pltpu.VMEM((1024, 128), LOW),
            pltpu.VMEM((1024, 128), LOW),
            pltpu.VMEM((128, 1024), LOW),
            pltpu.SemaphoreType.DMA((1,)),
        ],
        name="attention_stage",
        compiler_params=pltpu.CompilerParams(vmem_limit_bytes=GRANT),
        cost_estimate=pl.CostEstimate(
            flops=14 * 8 * 128**3, bytes_accessed=3 << 20, transcendentals=8 * 128 * 128
        ),
    )(*recv, upstream, segment_row)


def share_kernel(place, *refs):
    grads, blocks, turned, out = refs[:F], refs[F : F + T], refs[F + T], refs[F + T + 1]
    rows, radial = refs[-2:]
    for turn in range(F):
        target = pl.multiple_of(lax.rem(place[0] + F - turn, F) * 128, 128)
        rows[pl.ds(target, 128), :] = grads[turn][:, :1280]
        extra = grads[turn][:, 1280:].astype(WIDE)
        radial[pl.ds(target, 128), :] = jnp.broadcast_to(
            extra[:, :1] + extra[:, 1:2], (128, 128)
        )
    for turn in range(T):
        target = lax.rem(place[1] + turn, T)
        total = mm(rows[...], turned[feature_block(target)], (1, 0))
        scale = radial[...]
        for half in range(2):
            lanes = slice(128 * half, 128 * (half + 1))
            block = blocks[(T - turn) % T][:, lanes].astype(WIDE)
            out[target, :, lanes] = (total[:, lanes] - block * scale).astype(LOW)


def code_share_kernel(place, *refs):
    parts, columns, decoded_grad, code_share = refs[0], refs[1 : 1 + F], refs[-2], refs[-1]
    total = parts[0].astype(WIDE)
    for turn in range(1, T):
        total = total + parts[turn].astype(WIDE)
    low = total.astype(LOW)
    decoded_grad[...] = low
    y = place[1] // 2
    for turn in range(F):
        code_share[lax.rem(y + F - turn, F)] = mm(low, columns[turn][...], (1, 1)).astype(LOW)


def decoder_part_kernel(place, pieces, decoded_grad, *outs):
    y = place[1] // 2
    for turn in range(F):
        outs[turn][...] = mm(
            pieces[lax.rem(y + F - turn, F)], decoded_grad[...], (0, 0)
        ).astype(LOW)


def decoder_out_kernel(place, *refs):
    blocks, decoder_grad = refs[:F], refs[F]
    for turn in range(F):
        lane = pl.multiple_of(lax.rem(place[0] + turn, F) * 256, 256)
        decoder_grad[:, pl.ds(lane, 256)] = blocks[turn][...].astype(WIDE)


def encoder_grad_kernel(place, columns, *refs):
    hidden, encoder, encoder_grad, staged = refs[:F], refs[F : 2 * F], refs[2 * F], refs[2 * F + 1]
    for turn in range(F):
        row = pl.multiple_of(lax.rem(place[0] + F - turn, F) * 128, 128)
        part = mm(columns[pl.ds(row, 128), :], hidden[turn][...], (0, 0))
        if turn == 0:
            encoder_grad[...] = part
        else:
            encoder_grad[...] += part
        staged[turn] = encoder[turn][...]


def hidden_grad_kernel(place, *refs):
    rows, staged, hidden_grad = refs[:F], refs[F], refs[F + 1]
    total = mm(rows[0][...], staged[0], (1, 0))
    for turn in range(1, F):
        total = total + mm(rows[turn][...], staged[turn], (1, 0))
    hidden_grad[...] = total.astype(LOW)


def section_step(
    hidden,
    encoder_weight,
    decoder_weight,
    query_weight,
    key_weight,
    value_weight,
    segments,
    out_grad,
):
    f = lax.axis_index("fsdp")
    t = lax.axis_index("tensor")
    place = jnp.stack([f, t]).astype(jnp.int32)
    encoder = encoder_weight[0]
    decoder = decoder_weight[0]
    weights = (query_weight[0], key_weight[0], value_weight[0])

    hidden_parts = [hidden[0]]
    for turn in range(1, F):
        hidden_parts.append(around(hidden[0], "fsdp", F, turn))

    decoder_parts = []
    for turn in range(F):
        start = pl.multiple_of(lax.rem(f + turn, 4) * 256, 256)
        block = lax.dynamic_slice_in_dim(decoder, start, 256, 1)
        decoder_parts.append(lax.ppermute(block, FT, column_route(turn)))

    small = 2 * 512 * 1024 * 256
    own, turned_encoder = call(
        stage_code_kernel,
        [shape((128, 1024)), shape((1024, 256))],
        [place, hidden[0], encoder],
        0,
    )
    (code_part,) = call(
        code_kernel,
        [shape((512, 256))],
        [place, own, *hidden_parts[1:], turned_encoder],
        small,
        [pltpu.VMEM((512, 1024), LOW)],
    )
    came = exchange(code_part.reshape(T, 64, 256), "tensor")
    code_piece = jnp.sum(came.astype(WIDE), axis=0).astype(LOW)
    code_moved = to_section(code_piece, 1)
    pieces = spread(code_moved, FT, F * T).reshape(F, 512, 256)

    (decoded,) = call(
        decode_kernel, [shape((512, 256))], [place, pieces, *decoder_parts], small
    )
    blocks = [decoded]
    for turn in range(1, T):
        blocks.append(around(decoded, "tensor", T, turn))

    encoder, decoded = lax.optimization_barrier((encoder, decoded))
    encoder_parts = [encoder]
    for turn in range(1, F):
        encoder_parts.append(around(encoder, "fsdp", F, turn))

    turned, query, pair = stage_weights(*weights)
    sent = call(
        project_kernel,
        [shape((128, 1408))] * F,
        [place, *blocks, query, pair],
        10 * small,
        [pltpu.VMEM((512, 2048), LOW)],
    )
    came = [sent[0]]
    for turn in range(1, F):
        came.append(around(sent[turn], "fsdp", F, turn))
    mixed, sent = attention_stage(came, out_grad[0], segments[0])
    grads = [sent]
    for turn in range(1, F):
        grads.append(around(sent, "fsdp", F, turn))

    (share,) = call(
        share_kernel,
        [shape((T, 512, 256))],
        [place, *grads, *blocks, turned],
        10 * small,
        [pltpu.VMEM((512, 1280), LOW), pltpu.VMEM((512, 128), WIDE)],
    )
    parts = exchange(share, "tensor")
    decoded_grad, code_share = call(
        code_share_kernel,
        [shape((512, 256)), shape((F, 512, 256))],
        [place, parts, *decoder_parts],
        small,
    )
    came = exchange(code_share.reshape(F * T, 64, 256), FT)
    grad_piece = jnp.sum(came.astype(WIDE), axis=0).astype(LOW)
    grad_moved = to_section(grad_piece, -1)

    decoder_blocks = call(
        decoder_part_kernel,
        [shape((256, 256))] * F,
        [place, pieces, decoded_grad],
        small,
    )
    came = []
    for turn in range(F):
        back = [(target, source) for source, target in column_route(turn)]
        came.append(lax.ppermute(decoder_blocks[turn], FT, back))
    (decoder_grad,) = call(
        decoder_out_kernel, [shape((256, 1024), WIDE)], [place, *came], 0
    )

    code_grad = spread(grad_moved, "tensor", T).reshape(512, 256)
    grad_rows = []
    for turn in range(F):
        start = lax.rem(f + turn, F) * 128
        part = lax.dynamic_slice_in_dim(code_grad, start, 128, 0)
        grad_rows.append(around(part, "fsdp", F, turn) if turn else part)
    encoder_grad, staged = call(
        encoder_grad_kernel,
        [shape((256, 1024), WIDE), shape((F, 256, 1024))],
        [place, code_grad, *hidden_parts, *encoder_parts],
        small,
    )
    (hidden_grad,) = call(
        hidden_grad_kernel, [shape((128, 1024))], [place, *grad_rows, staged], small
    )
    return (mixed[None], hidden_grad[None], encoder_grad[None], decoder_grad[None])


def solution(mesh):
    placed = P("section", "fsdp", "tensor")
    return jax.shard_map(
        section_step,
        mesh=mesh,
        in_specs=(placed,) * 6 + (P("section", "fsdp", None), placed),
        out_specs=(placed,) * 4,
        check_vma=False,
    )
```
